512 devices in a mesh: img: 64 (over y, z), lm: 8 (over x, core).
Axes of the slice: x: 4, y: 4, z: 16, core: 2. Of those that a mesh axis runs over, the one named last changes fastest.
Arguments:
- jac_point: float32 [6, 1048576], P(None, ('img', 'lm')), may hold values from -4 to 4
- jac_cam: bfloat16 [1048576, 256], P(('img', 'lm')), may hold values from -0.125 to 0.125
- resid: float32 [2, 1048576], P(None, ('img', 'lm')), may hold values from -6 to 6
- point_ids: int32 [1048576], P(('img', 'lm')), may hold values from 0 to 4095
- cam_ids: int32 [1048576], P(('img', 'lm')), may hold values from 0 to 1023
- owner_slot: int32 [1024], replicated, may hold values from 0 to 1023, each once
- damping: float32 [1], replicated, may hold values from 0.1 to 1
Outputs:
- landmark_step: float32 [3, 32768], P(None, 'lm')
- camera_gradient: float32 [1024, 128], P(('img', 'lm'))
The draws below stay inside these ranges and needn't reach their ends.
All inputs are finite; a program needn't handle non-finite values.
Results may differ from the reference program's by a relative error of at most 0.0029.
Values sent between devices are 32-bit elements; how exact they have to be, the bound alone decides.
No kernel may reach another device: no remote copies, remote signals or barrier semaphores. Data moves between devices by JAX's collectives and lax.ppermute only.
A program may use at most 64 MiB of HBM per device.

```python
import math
import jax
import jax.numpy as jnp
import numpy as np
from jax import lax

CAMP = 128
BLOCK = 64
OBS_DEV = 2048
LM_BLOCKS = 64
GPD = 2
LANDMARKS = 32768
GROUPS = 1024
OBS = 1048576
N_LM = 8


def plant(result, rng, least, top_value):
    extent = result.shape
    place = [jax.random.randint(jax.random.fold_in(rng, axis), (), 0, extent[axis]) for axis in range(len(extent))]
    result = result.at[tuple(place)].set(least)
    longest = extent.index(max(extent))
    place[longest] = (place[longest] + 1) % extent[longest]
    return result.at[tuple(place)].set(top_value)


def levels(own_key, shape, pieces, low, high):
    def one(position, shards_of):
        draws = jax.random.uniform(jax.random.fold_in(jax.random.fold_in(own_key, 6), position), (shards_of,), jnp.float32, low / len(pieces), high / len(pieces))
        return jnp.repeat(jnp.exp(draws), shape[position] // shards_of).reshape((-1,) + (1,) * (len(shape) - position - 1))

    level = one(*pieces[0])
    for cut in pieces[1:]:
        level = level * one(*cut)
    return level


def cumulative_ranks(count, skew):
    portions = [(1 << 20) // math.isqrt(grade ** skew) + 1 for grade in range(1, count + 1)]
    scale = 1 + sum(portions) // (1 << 30)
    return np.cumsum(np.array([max(1, weight // scale) for weight in portions]))


def ranked(stream_key, extent, count, skew):
    listing = cumulative_ranks(count, skew)
    ticket = jax.random.randint(jax.random.fold_in(stream_key, 1), extent, 0, int(listing[count - 1]))
    standing = jnp.searchsorted(jnp.asarray(listing, jnp.int32), ticket, side="right")
    return jax.random.permutation(jax.random.fold_in(stream_key, 2), count)[standing].astype(jnp.int32)


def normal_values(key, shape, scale, limit, shards=(), kind=jnp.bfloat16):
    level = levels(key, shape, shards, -0.22, 0.18) if shards else 1.0
    entries = jax.random.normal(key, shape, jnp.float32) * scale * level
    return jnp.minimum(jnp.maximum(entries, -limit), limit).astype(kind)


def setup_inputs(seed: int = 0) -> dict:
    keys = jax.random.split(jax.random.key(seed), 8)
    return {
        "jac_point": normal_values(keys[0], (6, OBS), 0.25, 4.0, ((1, 512),), jnp.float32),
        "jac_cam": normal_values(keys[1], (OBS, 2 * CAMP), (2 * OBS_DEV // GPD) ** -0.5, 0.125, ((0, 512),)),
        "resid": normal_values(keys[2], (2, OBS), 1.0, 6.0, ((1, 512),), jnp.float32),
        "point_ids": plant(jax.random.randint(keys[3], (OBS,), 0, LM_BLOCKS * BLOCK), jax.random.fold_in(keys[3], 1), 0, (LM_BLOCKS * BLOCK) - 1).astype(jnp.int32),
        "cam_ids": plant(ranked(keys[4], (OBS,), GROUPS, 1), jax.random.fold_in(keys[4], 3), 0, GROUPS - 1).astype(jnp.int32),
        "owner_slot": jax.random.permutation(keys[5], GROUPS).astype(jnp.int32),
        "damping": jnp.clip(jnp.exp(jax.random.uniform(keys[6], (1,), jnp.float32, math.log(0.1), math.log(1.0))), 0.1, 1.0),
    }


def obs_terms(jac_point, resid):
    u0, u1, u2 = jac_point[0], jac_point[1], jac_point[2]
    v0, v1, v2 = jac_point[3], jac_point[4], jac_point[5]
    ru, rv = resid[0], resid[1]
    return jnp.stack([u0 * u0 + v0 * v0, u0 * u1 + v0 * v1, u0 * u2 + v0 * v2,
                      u1 * u1 + v1 * v1, u1 * u2 + v1 * v2, u2 * u2 + v2 * v2,
                      u0 * ru + v0 * rv, u1 * ru + v1 * rv, u2 * ru + v2 * rv], axis=1)


def solve_points(stats, damping):
    factor = damping[0]
    h01, h02, h12 = stats[1], stats[2], stats[4]
    a00 = stats[0] + factor * (stats[0] + 1.0)
    a11 = stats[3] + factor * (stats[3] + 1.0)
    a22 = stats[5] + factor * (stats[5] + 1.0)
    g0, g1, g2 = stats[6], stats[7], stats[8]
    c00 = a11 * a22 - h12 * h12
    c01 = h02 * h12 - h01 * a22
    c02 = h01 * h12 - h02 * a11
    c11 = a00 * a22 - h02 * h02
    c12 = h01 * h02 - a00 * h12
    c22 = a00 * a11 - h01 * h01
    determ = a00 * c00 + h01 * c01 + h02 * c02
    s0 = -(c00 * g0 + c01 * g1 + c02 * g2) / determ
    s1 = -(c01 * g0 + c11 * g1 + c12 * g2) / determ
    s2 = -(c02 * g0 + c12 * g1 + c22 * g2) / determ
    return jnp.stack([s0, s1, s2], axis=0)


def correct(jac_point, resid, step_obs):
    cu = resid[0] + jac_point[0] * step_obs[0] + jac_point[1] * step_obs[1] + jac_point[2] * step_obs[2]
    cv = resid[1] + jac_point[3] * step_obs[0] + jac_point[4] * step_obs[1] + jac_point[5] * step_obs[2]
    return cu, cv


def reference(jac_point, jac_cam, resid, point_ids, cam_ids, owner_slot, damping):
    total = point_ids.shape[0]
    slice_points = LM_BLOCKS * BLOCK
    rows = jnp.arange(total, dtype=jnp.int32)
    landmark = ((rows // OBS_DEV) % N_LM) * slice_points + point_ids
    terms = obs_terms(jac_point, resid)
    stats = jax.ops.segment_sum(terms, landmark, num_segments=LANDMARKS).T
    step = solve_points(stats, damping)
    cu, cv = correct(jac_point, resid, step[:, landmark])
    cu = lax.optimization_barrier(cu.astype(jnp.bfloat16)).astype(jnp.float32)
    cv = lax.optimization_barrier(cv.astype(jnp.bfloat16)).astype(jnp.float32)
    slots = owner_slot[cam_ids]
    devices = total // OBS_DEV
    cu_b = cu.reshape(devices, OBS_DEV)
    cv_b = cv.reshape(devices, OBS_DEV)
    cam_b = jac_cam.reshape(devices, OBS_DEV, 2 * CAMP)
    slot_b = slots.reshape(devices, OBS_DEV)

    def add_block(carry, items):
        bu, bv, bcam, bslot = items
        contrib = bu[:, None] * bcam[:, :CAMP].astype(jnp.float32) + bv[:, None] * bcam[:, CAMP:].astype(jnp.float32)
        return carry + jax.ops.segment_sum(contrib, bslot, num_segments=GROUPS), None

    init = jnp.zeros((GROUPS, CAMP), jnp.float32)
    gradient, _ = lax.scan(add_block, init, (cu_b, cv_b, cam_b, slot_b))
    return step, gradient
```

```python
import jax
import jax.numpy as jnp
from jax import lax
from jax.sharding import Mesh
from jax.sharding import PartitionSpec as P

CAMP = 128
BLOCK = 64
LM_BLOCKS = 64


def obs_terms(jac_point, resid):
    u0, u1, u2 = (jac_point[0], jac_point[1], jac_point[2])
    v0, v1, v2 = (jac_point[3], jac_point[4], jac_point[5])
    ru, rv = (resid[0], resid[1])
    return jnp.stack(
        [
            u0 * u0 + v0 * v0,
            u0 * u1 + v0 * v1,
            u0 * u2 + v0 * v2,
            u1 * u1 + v1 * v1,
            u1 * u2 + v1 * v2,
            u2 * u2 + v2 * v2,
            u0 * ru + v0 * rv,
            u1 * ru + v1 * rv,
            u2 * ru + v2 * rv,
        ],
        axis=1,
    )


def solve_points(stats, damping):
    factor = damping[0]
    h01, h02, h12 = (stats[1], stats[2], stats[4])
    a00 = stats[0] + factor * (stats[0] + 1.0)
    a11 = stats[3] + factor * (stats[3] + 1.0)
    a22 = stats[5] + factor * (stats[5] + 1.0)
    g0, g1, g2 = (stats[6], stats[7], stats[8])
    c00 = a11 * a22 - h12 * h12
    c01 = h02 * h12 - h01 * a22
    c02 = h01 * h12 - h02 * a11
    c11 = a00 * a22 - h02 * h02
    c12 = h01 * h02 - a00 * h12
    c22 = a00 * a11 - h01 * h01
    determ = a00 * c00 + h01 * c01 + h02 * c02
    s0 = -(c00 * g0 + c01 * g1 + c02 * g2) / determ
    s1 = -(c01 * g0 + c11 * g1 + c12 * g2) / determ
    s2 = -(c02 * g0 + c12 * g1 + c22 * g2) / determ
    return jnp.stack([s0, s1, s2], axis=0)


IMG = ("y", "z")
LM = ("x", "c")
ALL = ("y", "z", "x", "c")


def per_device(jac_point, jac_cam, resid, point_ids, cam_ids, owner_slot, damping):
    slice_points = LM_BLOCKS * BLOCK
    terms = obs_terms(jac_point, resid)
    local_stats = jax.ops.segment_sum(terms, point_ids, num_segments=slice_points).T
    parts = local_stats.reshape(9, 64, BLOCK).transpose(1, 0, 2)
    parts = lax.all_to_all(parts, IMG, 0, 0)
    own_step = solve_points(jnp.sum(parts, axis=0), damping)
    steps = lax.all_to_all(jnp.broadcast_to(own_step, (64, 3, BLOCK)), IMG, 0, 0)
    step = steps.transpose(1, 0, 2).reshape(3, slice_points)
    step_obs = jnp.take(step, point_ids, axis=1)
    cu = (
        resid[0]
        + jac_point[0] * step_obs[0]
        + jac_point[1] * step_obs[1]
        + jac_point[2] * step_obs[2]
    )
    cv = (
        resid[1]
        + jac_point[3] * step_obs[0]
        + jac_point[4] * step_obs[1]
        + jac_point[5] * step_obs[2]
    )
    cu_half = cu.astype(jnp.bfloat16)
    cv_half = cv.astype(jnp.bfloat16)
    row = owner_slot
    y, z, x, c, g = row // 256, (row // 16) % 16, (row // 4) % 4, (row // 2) % 2, row % 2
    place = ((y * 4 + x) * 2 + c) * 32 + z * 2 + g
    slots = jnp.take(place, cam_ids)
    groups_all = owner_slot.shape[0]
    n_obs = cam_ids.shape[0]
    width = min(1024, n_obs)
    group_iota = jnp.arange(groups_all, dtype=jnp.int32)[:, None]
    partial_grad = jnp.zeros((groups_all, CAMP), jnp.float32)
    for block_index in range(n_obs // width):
        lo_row = block_index * width
        block_slots = slots[lo_row : lo_row + width]
        member = (block_slots[None, :] == group_iota).astype(jnp.bfloat16)
        left_u = member * cu_half[None, lo_row : lo_row + width]
        left_v = member * cv_half[None, lo_row : lo_row + width]
        cam_block = jac_cam[lo_row : lo_row + width]
        partial_grad = partial_grad + jnp.dot(
            left_u, cam_block[:, :CAMP], preferred_element_type=jnp.float32
        )
        partial_grad = partial_grad + jnp.dot(
            left_v, cam_block[:, CAMP:], preferred_element_type=jnp.float32
        )
    near = lax.all_to_all(partial_grad.reshape(32, 32, CAMP), ("y", "x", "c"), 0, 0)
    near = jnp.sum(near, axis=0)
    far = lax.all_to_all(near.reshape(16, 2, CAMP), "z", 0, 0)
    return (step, jnp.sum(far, axis=0))


def solution(mesh):
    torus = Mesh(mesh.devices.reshape(4, 16, 4, 2), ALL)
    placed = (
        P(None, ALL),
        P(ALL, None),
        P(None, ALL),
        P(ALL),
        P(ALL),
        P(),
        P(),
    )
    return jax.shard_map(
        per_device,
        mesh=torus,
        in_specs=placed,
        out_specs=(P(None, LM), P(ALL, None)),
        check_vma=False,
    )
```

```python
import jax
import jax.numpy as jnp
from jax import lax
from jax.experimental import pallas as pl
from jax.experimental.pallas import tpu as pltpu
from jax.sharding import Mesh
from jax.sharding import PartitionSpec as P

CAMP = 128
IMG = ("y", "z")
LM = ("x", "c")
ALL = ("y", "z", "x", "c")
NEAR = ("y", "x", "c")
F32 = jnp.float32
BF16 = jnp.bfloat16

LOWS = 16
HIGHS = 256
OWNERS = 64
OWNED = 64
NT = (((1,), (1,)), ((), ()))


def split(value):
    top = value.astype(BF16).astype(F32)
    return top, value - top


def row_of(ref):
    return jnp.concatenate([ref[i : i + 1, :] for i in range(ref.shape[0])], axis=1)


def one_hot(row, count):
    index = lax.broadcasted_iota(jnp.int32, (count, row.shape[1]), 0)
    return jnp.where(index == row, 1.0, 0.0).astype(BF16)


def swap_halves(value):
    return pltpu.roll(value, 64, 1)


def low_lanes(shape):
    return lax.broadcasted_iota(jnp.int32, shape, 1) < 64


def stats_kernel(jac_ref, res_ref, pid_ref, out_ref, hot_ref, terms_ref):
    pid = row_of(pid_ref)
    hot_ref[...] = one_hot(pid & 255, HIGHS)
    low = lax.shift_right_logical(pid, 8)
    u = [jac_ref[a : a + 1, :] for a in range(3)]
    v = [jac_ref[a : a + 1, :] for a in range(3, 6)]
    ru, rv = res_ref[0:1, :], res_ref[1:2, :]
    terms = [u[a] * u[b] + v[a] * v[b] for a, b in ((0, 0), (0, 1), (0, 2), (1, 1), (1, 2), (2, 2))]
    terms += [u[a] * ru + v[a] * rv for a in range(3)]
    member = lax.broadcasted_iota(jnp.int32, (LOWS, pid.shape[1]), 0) == low
    for i, term in enumerate(terms):
        for j, piece in enumerate(split(term)):
            at = (j * 9 + i) * LOWS
            terms_ref[at : at + LOWS, :] = jnp.where(member, piece, 0.0).astype(BF16)
    both = lax.dot_general(terms_ref[...], hot_ref[...], NT, preferred_element_type=F32)
    stats = both[: 9 * LOWS] + both[9 * LOWS :]
    first = low_lanes((LOWS, 128))
    for j in range(5):
        for k in range(4):
            lanes = slice((k // 2) * 128, (k // 2) * 128 + 128)
            one = stats[2 * j * LOWS : (2 * j + 1) * LOWS, lanes]
            if j < 4:
                two = stats[(2 * j + 1) * LOWS : (2 * j + 2) * LOWS, lanes]
            else:
                two = jnp.zeros_like(one)
            if k % 2:
                piece = jnp.where(first, swap_halves(one), two)
            else:
                piece = jnp.where(first, one, swap_halves(two))
            out_ref[k * LOWS : (k + 1) * LOWS, 0, j * 128 : (j + 1) * 128] = piece


def prepare_kernel(pid_ref, cam_ref, slot_ref, jac_ref, hot_ref, place_ref, turned_ref):
    hot_ref[...] = one_hot(row_of(pid_ref) & 255, HIGHS)
    cam = row_of(cam_ref)
    hot = one_hot(cam & 127, 128)
    slot = slot_ref[...]
    y, z, x = slot >> 8, (slot >> 4) & 15, (slot >> 1) & 7
    above, below = y * 8 + x, z * 2 + (slot & 1)
    table = jnp.concatenate([above, below], axis=0).astype(F32).astype(BF16)
    found = jnp.dot(table, hot, preferred_element_type=F32)
    member = lax.broadcasted_iota(jnp.int32, (8, cam.shape[1]), 0) == (cam >> 7)
    places = jnp.where(member, found[:8] * 32.0 + found[8:], 0.0)
    place_ref[...] = jnp.sum(places, axis=0, keepdims=True).astype(jnp.int32)
    turned_ref[...] = jac_ref[...].T


def solve_kernel(damp_ref, parts_ref, out_ref):
    total = parts_ref[0]
    for i in range(1, OWNERS):
        total = total + parts_ref[i]
    s = []
    for v in range(9):
        chunk = total[:, (v // 2) * 128 : (v // 2) * 128 + 128]
        s.append(swap_halves(chunk) if v % 2 else chunk)
    factor = damp_ref[...]
    h01, h02, h12 = s[1], s[2], s[4]
    a00 = s[0] + factor * (s[0] + 1.0)
    a11 = s[3] + factor * (s[3] + 1.0)
    a22 = s[5] + factor * (s[5] + 1.0)
    g0, g1, g2 = s[6], s[7], s[8]
    c00 = a11 * a22 - h12 * h12
    c01 = h02 * h12 - h01 * a22
    c02 = h01 * h12 - h02 * a11
    c11 = a00 * a22 - h02 * h02
    c12 = h01 * h02 - a00 * h12
    c22 = a00 * a11 - h01 * h01
    determ = a00 * c00 + h01 * c01 + h02 * c02
    s0 = -(c00 * g0 + c01 * g1 + c02 * g2) / determ
    s1 = -(c01 * g0 + c11 * g1 + c12 * g2) / determ
    s2 = -(c02 * g0 + c12 * g1 + c22 * g2) / determ
    first = low_lanes((1, 128))
    one = jnp.where(first, s0, swap_halves(s1))
    two = jnp.where(first, s2, 0.0)
    out_ref[...] = jnp.broadcast_to(jnp.concatenate([one, two], axis=1)[None], out_ref.shape)


def camera_kernel(
    steps_ref, jac_ref, res_ref, pid_ref, hot_ref, place_ref, turned_ref, step_ref, grad_ref, right_ref, left_ref
):
    blocks = [steps_ref[k * LOWS : (k + 1) * LOWS, 0, :] for k in range(4)]
    first = low_lanes((LOWS, 128))
    rows = []
    for axis in range(3):
        halves = []
        for kk in range(2):
            at = (axis // 2) * 128
            one, two = blocks[2 * kk][:, at : at + 128], blocks[2 * kk + 1][:, at : at + 128]
            if axis % 2:
                halves.append(jnp.where(first, swap_halves(one), two))
            else:
                halves.append(jnp.where(first, one, swap_halves(two)))
        rows.append(jnp.concatenate(halves, axis=1))
    for axis in range(3):
        for low in range(LOWS):
            step_ref[axis : axis + 1, low * HIGHS : (low + 1) * HIGHS] = rows[axis][low : low + 1, :]
    table = jnp.concatenate(rows, axis=0)
    top, rest = split(table)
    table = jnp.concatenate([top, rest], axis=0).astype(BF16)
    found = jnp.dot(table, hot_ref[...], preferred_element_type=F32)
    found = found[: 3 * LOWS] + found[3 * LOWS :]
    pid = row_of(pid_ref)
    member = lax.broadcasted_iota(jnp.int32, (LOWS, pid.shape[1]), 0) == lax.shift_right_logical(pid, 8)
    s = [
        jnp.sum(jnp.where(member, found[a * LOWS : (a + 1) * LOWS], 0.0), axis=0, keepdims=True)
        for a in range(3)
    ]
    cu = res_ref[0:1, :] + jac_ref[0:1, :] * s[0] + jac_ref[1:2, :] * s[1] + jac_ref[2:3, :] * s[2]
    cv = res_ref[1:2, :] + jac_ref[3:4, :] * s[0] + jac_ref[4:5, :] * s[1] + jac_ref[5:6, :] * s[2]
    cu = cu.astype(BF16).astype(F32)
    cv = cv.astype(BF16).astype(F32)
    terms = turned_ref[:CAMP, :].astype(F32) * cu + turned_ref[CAMP:, :].astype(F32) * cv
    top, rest = split(terms)
    right_ref[:CAMP, :] = top.astype(BF16)
    right_ref[CAMP:, :] = rest.astype(BF16)
    place = place_ref[...]
    for q in range(grad_ref.shape[0] // 256):
        left_ref[...] = one_hot(place - q * 256, 256)
        both = lax.dot_general(left_ref[...], right_ref[...], NT, preferred_element_type=F32)
        grad_ref[q * 256 : (q + 1) * 256, :] = both[:, :CAMP] + both[:, CAMP:]


def shape(dims, kind=F32):
    return jax.ShapeDtypeStruct(dims, kind)


LIMIT = pltpu.CompilerParams(vmem_limit_bytes=16 * 1024 * 1024)


def cost(flops, size):
    return pl.CostEstimate(flops=flops, bytes_accessed=size, transcendentals=0)


def per_device(jac_point, jac_cam, resid, point_ids, cam_ids, owner_slot, damping):
    count = point_ids.shape[0]
    groups = owner_slot.shape[0]
    points = LOWS * HIGHS
    vmem = pl.BlockSpec(memory_space=pltpu.VMEM)
    pids = point_ids.reshape(count // 128, 128)
    cams = cam_ids.reshape(count // 128, 128)
    parts = pl.pallas_call(
        stats_kernel,
        out_shape=shape((OWNERS, 1, 640)),
        in_specs=[vmem] * 3,
        out_specs=vmem,
        scratch_shapes=[pltpu.VMEM((HIGHS, count), BF16), pltpu.VMEM((18 * LOWS, count), BF16)],
        name="stats",
    )(jac_point, resid, pids)
    parts = lax.all_to_all(parts, IMG, 0, 0, tiled=True)
    hot, place, turned = pl.pallas_call(
        prepare_kernel,
        out_shape=(shape((HIGHS, count), BF16), shape((1, count), jnp.int32), shape((2 * CAMP, count), BF16)),
        in_specs=[vmem] * 4,
        out_specs=(vmem, vmem, vmem),
        cost_estimate=cost(10_000_000, 6_000_000),
        compiler_params=LIMIT,
        name="prepare",
    )(pids, cams, owner_slot.reshape(8, groups // 8), jac_cam)
    steps = pl.pallas_call(
        solve_kernel,
        out_shape=shape((OWNERS, 1, 256)),
        in_specs=[vmem, vmem],
        out_specs=vmem,
        compiler_params=LIMIT,
        name="solve",
    )(damping.reshape(1, 1), parts)
    steps = lax.all_to_all(steps, IMG, 0, 0, tiled=True)
    step, partial_grad = pl.pallas_call(
        camera_kernel,
        out_shape=(shape((3, points)), shape((groups, CAMP))),
        in_specs=[vmem] * 7,
        out_specs=(vmem, vmem),
        scratch_shapes=[pltpu.VMEM((2 * CAMP, count), BF16), pltpu.VMEM((256, count), BF16)],
        compiler_params=LIMIT,
        name="camera",
    )(steps, jac_point, resid, pids, hot, place, turned)
    near = lax.all_to_all(partial_grad.reshape(32, 32, CAMP), NEAR, 0, 0, tiled=True)
    near = jnp.sum(near, axis=0)
    far = lax.all_to_all(near.reshape(16, 2, CAMP), "z", 0, 0, tiled=True)
    return (step, jnp.sum(far, axis=0))


def solution(mesh):
    torus = Mesh(mesh.devices.reshape(4, 16, 4, 2), ALL)
    placed = (
        P(None, ALL),
        P(ALL, None),
        P(None, ALL),
        P(ALL),
        P(ALL),
        P(),
        P(),
    )
    return jax.shard_map(
        per_device,
        mesh=torus,
        in_specs=placed,
        out_specs=(P(None, LM), P(ALL, None)),
        check_vma=False,
    )
```

```python
import jax
import jax.numpy as jnp
import numpy as np
from jax import lax
from jax.experimental import pallas as pl
from jax.experimental.pallas import tpu as pltpu
from jax.sharding import Mesh
from jax.sharding import PartitionSpec as P

CAMP = 128
IMG = ("y", "z")
LM = ("x", "c")
ALL = ("y", "z", "x", "c")
FLAT = ("img", "lm")
GRID = np.arange(512).reshape(4, 16, 4, 2)
TURNED = GRID[[2, 3, 0, 1]][:, [z ^ 8 for z in range(16)]][:, :, [2, 3, 0, 1]]
IMG_GROUPS = [TURNED[:, :, x, c].reshape(-1).tolist() for x in range(4) for c in range(2)]
NEAR_GROUPS = [TURNED[:, z].reshape(-1).tolist() for z in range(16)]
FAR_GROUPS = [TURNED[y, :, x, c].tolist() for y in range(4) for x in range(4) for c in range(2)]
F32 = jnp.float32
BF16 = jnp.bfloat16

LOWS = 16
HIGHS = 256
OWNERS = 64
OWNED = 64
NT = (((1,), (1,)), ((), ()))


def split(value):
    top = value.astype(BF16).astype(F32)
    return top, value - top


def row_of(ref):
    return jnp.concatenate([ref[i : i + 1, :] for i in range(ref.shape[0])], axis=1)


def one_hot(row, count):
    index = lax.broadcasted_iota(jnp.int32, (count, row.shape[1]), 0)
    return jnp.where(index == row, 1.0, 0.0).astype(BF16)


def swap_halves(value):
    return pltpu.roll(value, 64, 1)


def low_lanes(shape):
    return lax.broadcasted_iota(jnp.int32, shape, 1) < 64


def stats_kernel(jac_ref, res_ref, pid_ref, out_ref, hot_ref, terms_ref):
    pid = row_of(pid_ref)
    hot_ref[...] = one_hot(pid & 255, HIGHS)
    low = lax.shift_right_logical(pid, 8)
    u = [jac_ref[a : a + 1, :] for a in range(3)]
    v = [jac_ref[a : a + 1, :] for a in range(3, 6)]
    ru, rv = res_ref[0:1, :], res_ref[1:2, :]
    terms = [u[a] * u[b] + v[a] * v[b] for a, b in ((0, 0), (0, 1), (0, 2), (1, 1), (1, 2), (2, 2))]
    terms += [u[a] * ru + v[a] * rv for a in range(3)]
    member = lax.broadcasted_iota(jnp.int32, (LOWS, pid.shape[1]), 0) == low
    for i, term in enumerate(terms):
        for j, piece in enumerate(split(term)):
            at = (j * 9 + i) * LOWS
            terms_ref[at : at + LOWS, :] = jnp.where(member, piece, 0.0).astype(BF16)
    both = lax.dot_general(terms_ref[...], hot_ref[...], NT, preferred_element_type=F32)
    stats = both[: 9 * LOWS] + both[9 * LOWS :]
    first = low_lanes((LOWS, 128))
    for j in range(5):
        for k in range(4):
            lanes = slice((k // 2) * 128, (k // 2) * 128 + 128)
            one = stats[2 * j * LOWS : (2 * j + 1) * LOWS, lanes]
            if j < 4:
                two = stats[(2 * j + 1) * LOWS : (2 * j + 2) * LOWS, lanes]
            else:
                two = jnp.zeros_like(one)
            if k % 2:
                piece = jnp.where(first, swap_halves(one), two)
            else:
                piece = jnp.where(first, one, swap_halves(two))
            out_ref[k * LOWS : (k + 1) * LOWS, 0, j * 128 : (j + 1) * 128] = piece


def prepare_kernel(pid_ref, cam_ref, slot_ref, jac_ref, hot_ref, place_ref, turned_ref):
    hot_ref[...] = one_hot(row_of(pid_ref) & 255, HIGHS)
    cam = row_of(cam_ref)
    hot = one_hot(cam & 127, 128)
    slot = slot_ref[...]
    y, z, x = (slot >> 8) ^ 2, ((slot >> 4) & 15) ^ 8, ((slot >> 1) & 7) ^ 4
    above, below = y * 8 + x, z * 2 + (slot & 1)
    table = jnp.concatenate([above, below], axis=0).astype(F32).astype(BF16)
    found = jnp.dot(table, hot, preferred_element_type=F32)
    member = lax.broadcasted_iota(jnp.int32, (8, cam.shape[1]), 0) == (cam >> 7)
    places = jnp.where(member, found[:8] * 32.0 + found[8:], 0.0)
    place_ref[...] = jnp.sum(places, axis=0, keepdims=True).astype(jnp.int32)
    turned_ref[...] = jac_ref[...].T


def solve_kernel(damp_ref, parts_ref, out_ref):
    total = parts_ref[0]
    for i in range(1, OWNERS):
        total = total + parts_ref[i]
    s = []
    for v in range(9):
        chunk = total[:, (v // 2) * 128 : (v // 2) * 128 + 128]
        s.append(swap_halves(chunk) if v % 2 else chunk)
    factor = damp_ref[...]
    h01, h02, h12 = s[1], s[2], s[4]
    a00 = s[0] + factor * (s[0] + 1.0)
    a11 = s[3] + factor * (s[3] + 1.0)
    a22 = s[5] + factor * (s[5] + 1.0)
    g0, g1, g2 = s[6], s[7], s[8]
    c00 = a11 * a22 - h12 * h12
    c01 = h02 * h12 - h01 * a22
    c02 = h01 * h12 - h02 * a11
    c11 = a00 * a22 - h02 * h02
    c12 = h01 * h02 - a00 * h12
    c22 = a00 * a11 - h01 * h01
    determ = a00 * c00 + h01 * c01 + h02 * c02
    s0 = -(c00 * g0 + c01 * g1 + c02 * g2) / determ
    s1 = -(c01 * g0 + c11 * g1 + c12 * g2) / determ
    s2 = -(c02 * g0 + c12 * g1 + c22 * g2) / determ
    first = low_lanes((1, 128))
    one = jnp.where(first, s0, swap_halves(s1))
    two = jnp.where(first, s2, 0.0)
    out_ref[...] = jnp.broadcast_to(jnp.concatenate([one, two], axis=1)[None], out_ref.shape)


def camera_kernel(
    steps_ref, jac_ref, res_ref, pid_ref, hot_ref, place_ref, turned_ref, step_ref, grad_ref, right_ref, left_ref
):
    blocks = [steps_ref[k * LOWS : (k + 1) * LOWS, 0, :] for k in range(4)]
    first = low_lanes((LOWS, 128))
    rows = []
    for axis in range(3):
        halves = []
        for kk in range(2):
            at = (axis // 2) * 128
            one, two = blocks[2 * kk][:, at : at + 128], blocks[2 * kk + 1][:, at : at + 128]
            if axis % 2:
                halves.append(jnp.where(first, swap_halves(one), two))
            else:
                halves.append(jnp.where(first, one, swap_halves(two)))
        rows.append(jnp.concatenate(halves, axis=1))
    for axis in range(3):
        for low in range(LOWS):
            step_ref[axis : axis + 1, low * HIGHS : (low + 1) * HIGHS] = rows[axis][low : low + 1, :]
    table = jnp.concatenate(rows, axis=0)
    top, rest = split(table)
    table = jnp.concatenate([top, rest], axis=0).astype(BF16)
    found = jnp.dot(table, hot_ref[...], preferred_element_type=F32)
    found = found[: 3 * LOWS] + found[3 * LOWS :]
    pid = row_of(pid_ref)
    member = lax.broadcasted_iota(jnp.int32, (LOWS, pid.shape[1]), 0) == lax.shift_right_logical(pid, 8)
    s = [
        jnp.sum(jnp.where(member, found[a * LOWS : (a + 1) * LOWS], 0.0), axis=0, keepdims=True)
        for a in range(3)
    ]
    cu = res_ref[0:1, :] + jac_ref[0:1, :] * s[0] + jac_ref[1:2, :] * s[1] + jac_ref[2:3, :] * s[2]
    cv = res_ref[1:2, :] + jac_ref[3:4, :] * s[0] + jac_ref[4:5, :] * s[1] + jac_ref[5:6, :] * s[2]
    cu = cu.astype(BF16).astype(F32)
    cv = cv.astype(BF16).astype(F32)
    terms = turned_ref[:CAMP, :].astype(F32) * cu + turned_ref[CAMP:, :].astype(F32) * cv
    top, rest = split(terms)
    right_ref[:CAMP, :] = top.astype(BF16)
    right_ref[CAMP:, :] = rest.astype(BF16)
    place = place_ref[...]
    for q in range(grad_ref.shape[0] // 256):
        left_ref[...] = one_hot(place - q * 256, 256)
        both = lax.dot_general(left_ref[...], right_ref[...], NT, preferred_element_type=F32)
        grad_ref[q * 256 : (q + 1) * 256, :] = both[:, :CAMP] + both[:, CAMP:]


def shape(dims, kind=F32):
    return jax.ShapeDtypeStruct(dims, kind)


LIMIT = pltpu.CompilerParams(vmem_limit_bytes=16 * 1024 * 1024)


def cost(flops, size):
    return pl.CostEstimate(flops=flops, bytes_accessed=size, transcendentals=0)


def exchange(value, groups):
    return lax.all_to_all(value, FLAT, 0, 0, axis_index_groups=groups, tiled=True)


def per_device(jac_point, jac_cam, resid, point_ids, cam_ids, owner_slot, damping):
    count = point_ids.shape[0]
    groups = owner_slot.shape[0]
    points = LOWS * HIGHS
    vmem = pl.BlockSpec(memory_space=pltpu.VMEM)
    pids = point_ids.reshape(count // 128, 128)
    cams = cam_ids.reshape(count // 128, 128)
    parts = pl.pallas_call(
        stats_kernel,
        out_shape=shape((OWNERS, 1, 640)),
        in_specs=[vmem] * 3,
        out_specs=vmem,
        scratch_shapes=[pltpu.VMEM((HIGHS, count), BF16), pltpu.VMEM((18 * LOWS, count), BF16)],
        name="stats",
    )(jac_point, resid, pids)
    parts = exchange(parts, IMG_GROUPS)
    hot, place, turned = pl.pallas_call(
        prepare_kernel,
        out_shape=(shape((HIGHS, count), BF16), shape((1, count), jnp.int32), shape((2 * CAMP, count), BF16)),
        in_specs=[vmem] * 4,
        out_specs=(vmem, vmem, vmem),
        cost_estimate=cost(10_000_000, 6_000_000),
        compiler_params=LIMIT,
        name="prepare",
    )(pids, cams, owner_slot.reshape(8, groups // 8), jac_cam)
    steps = pl.pallas_call(
        solve_kernel,
        out_shape=shape((OWNERS, 1, 256)),
        in_specs=[vmem, vmem],
        out_specs=vmem,
        compiler_params=LIMIT,
        name="solve",
    )(damping.reshape(1, 1), parts)
    steps = exchange(steps, IMG_GROUPS)
    step, partial_grad = pl.pallas_call(
        camera_kernel,
        out_shape=(shape((3, points)), shape((groups, CAMP))),
        in_specs=[vmem] * 7,
        out_specs=(vmem, vmem),
        scratch_shapes=[pltpu.VMEM((2 * CAMP, count), BF16), pltpu.VMEM((256, count), BF16)],
        compiler_params=LIMIT,
        name="camera",
    )(steps, jac_point, resid, pids, hot, place, turned)
    near = exchange(partial_grad.reshape(32, 32, CAMP), NEAR_GROUPS)
    near = jnp.sum(near, axis=0)
    far = exchange(near.reshape(16, 2, CAMP), FAR_GROUPS)
    return (step, jnp.sum(far, axis=0))


def solution(mesh):
    placed = (P(None, FLAT), P(FLAT, None), P(None, FLAT), P(FLAT), P(FLAT), P(), P())
    return jax.shard_map(
        per_device,
        mesh=mesh,
        in_specs=placed,
        out_specs=(P(None, "lm"), P(FLAT, None)),
        check_vma=False,
    )
```

```python
import jax
import jax.numpy as jnp
import numpy as np
from jax import lax
from jax.experimental import pallas as pl
from jax.experimental.pallas import tpu as pltpu
from jax.sharding import Mesh
from jax.sharding import PartitionSpec as P

CAMP = 128
IMG = ("y", "z")
LM = ("x", "c")
ALL = ("y", "z", "x", "c")
FLAT = ("img", "lm")
GRID = np.arange(512).reshape(4, 16, 4, 2)
TURNED = GRID[[2, 3, 0, 1]][:, [z ^ 8 for z in range(16)]][:, :, [2, 3, 0, 1]]
PAIRS = TURNED.reshape(4, 8, 2, 4, 2)
CLOSE_GROUPS = [PAIRS[:, z, :, x, c].reshape(-1).tolist() for z in range(8) for x in range(4) for c in range(2)]
LINE_GROUPS = [PAIRS[y, :, z, x, c].tolist() for y in range(4) for z in range(2) for x in range(4) for c in range(2)]
NEAR_GROUPS = [TURNED[:, z].reshape(-1).tolist() for z in range(16)]
FAR_GROUPS = [TURNED[y, :, x, c].tolist() for y in range(4) for x in range(4) for c in range(2)]
F32 = jnp.float32
BF16 = jnp.bfloat16

LOWS = 16
HIGHS = 256
OWNERS = 8
OWNED = 512
NT = (((1,), (1,)), ((), ()))


def split(value):
    top = value.astype(BF16).astype(F32)
    return top, value - top


def row_of(ref):
    return jnp.concatenate([ref[i : i + 1, :] for i in range(ref.shape[0])], axis=1)


def one_hot(row, count):
    index = lax.broadcasted_iota(jnp.int32, (count, row.shape[1]), 0)
    return jnp.where(index == row, 1.0, 0.0).astype(BF16)


def stats_kernel(jac_ref, res_ref, pid_ref, out_ref, hot_ref, terms_ref):
    pid = row_of(pid_ref)
    hot_ref[...] = one_hot(pid & 255, HIGHS)
    low = lax.shift_right_logical(pid, 8)
    u = [jac_ref[a : a + 1, :] for a in range(3)]
    v = [jac_ref[a : a + 1, :] for a in range(3, 6)]
    ru, rv = res_ref[0:1, :], res_ref[1:2, :]
    terms = [u[a] * u[b] + v[a] * v[b] for a, b in ((0, 0), (0, 1), (0, 2), (1, 1), (1, 2), (2, 2))]
    terms += [u[a] * ru + v[a] * rv for a in range(3)]
    member = lax.broadcasted_iota(jnp.int32, (LOWS, pid.shape[1]), 0) == low
    for i, term in enumerate(terms):
        for j, piece in enumerate(split(term)):
            at = (j * 9 + i) * LOWS
            terms_ref[at : at + LOWS, :] = jnp.where(member, piece, 0.0).astype(BF16)
    both = lax.dot_general(terms_ref[...], hot_ref[...], NT, preferred_element_type=F32)
    stats = both[: 9 * LOWS] + both[9 * LOWS :]
    for v in range(9):
        for low in range(LOWS):
            at = v * OWNED + (low % 2) * HIGHS
            row = v * LOWS + low
            out_ref[low // 2, :, at : at + HIGHS] = stats[row : row + 1, :]


def prepare_kernel(pid_ref, cam_ref, slot_ref, jac_ref, hot_ref, place_ref, turned_ref):
    hot_ref[...] = one_hot(row_of(pid_ref) & 255, HIGHS)
    cam = row_of(cam_ref)
    hot = one_hot(cam & 127, 128)
    slot = slot_ref[...]
    y, z, x = (slot >> 8) ^ 2, ((slot >> 4) & 15) ^ 8, ((slot >> 1) & 7) ^ 4
    above, below = y * 8 + x, z * 2 + (slot & 1)
    table = jnp.concatenate([above, below], axis=0).astype(F32).astype(BF16)
    found = jnp.dot(table, hot, preferred_element_type=F32)
    member = lax.broadcasted_iota(jnp.int32, (8, cam.shape[1]), 0) == (cam >> 7)
    places = jnp.where(member, found[:8] * 32.0 + found[8:], 0.0)
    place_ref[...] = jnp.sum(places, axis=0, keepdims=True).astype(jnp.int32)
    turned_ref[...] = jac_ref[...].T


def total_of(parts_ref):
    total = parts_ref[0]
    for i in range(1, OWNERS):
        total = total + parts_ref[i]
    return total


def gather_kernel(parts_ref, out_ref):
    out_ref[...] = jnp.broadcast_to(total_of(parts_ref)[None], out_ref.shape)


def solve_kernel(damp_ref, parts_ref, out_ref):
    total = total_of(parts_ref)
    s = [total[:, v * OWNED : (v + 1) * OWNED] for v in range(9)]
    factor = damp_ref[...]
    h01, h02, h12 = s[1], s[2], s[4]
    a00 = s[0] + factor * (s[0] + 1.0)
    a11 = s[3] + factor * (s[3] + 1.0)
    a22 = s[5] + factor * (s[5] + 1.0)
    g0, g1, g2 = s[6], s[7], s[8]
    c00 = a11 * a22 - h12 * h12
    c01 = h02 * h12 - h01 * a22
    c02 = h01 * h12 - h02 * a11
    c11 = a00 * a22 - h02 * h02
    c12 = h01 * h02 - a00 * h12
    c22 = a00 * a11 - h01 * h01
    determ = a00 * c00 + h01 * c01 + h02 * c02
    s0 = -(c00 * g0 + c01 * g1 + c02 * g2) / determ
    s1 = -(c01 * g0 + c11 * g1 + c12 * g2) / determ
    s2 = -(c02 * g0 + c12 * g1 + c22 * g2) / determ
    out_ref[...] = jnp.broadcast_to(jnp.concatenate([s0, s1, s2], axis=1)[None], out_ref.shape)


def camera_kernel(
    steps_ref, jac_ref, res_ref, pid_ref, hot_ref, place_ref, turned_ref, step_ref, grad_ref, right_ref, left_ref, table_ref
):
    for axis in range(3):
        for low in range(LOWS):
            at = axis * OWNED + (low % 2) * HIGHS
            row = steps_ref[low // 2, :, at : at + HIGHS]
            table_ref[axis * LOWS + low : axis * LOWS + low + 1, :] = row
            step_ref[axis : axis + 1, low * HIGHS : (low + 1) * HIGHS] = row
    table = table_ref[...]
    top, rest = split(table)
    table = jnp.concatenate([top, rest], axis=0).astype(BF16)
    found = jnp.dot(table, hot_ref[...], preferred_element_type=F32)
    found = found[: 3 * LOWS] + found[3 * LOWS :]
    pid = row_of(pid_ref)
    member = lax.broadcasted_iota(jnp.int32, (LOWS, pid.shape[1]), 0) == lax.shift_right_logical(pid, 8)
    s = [
        jnp.sum(jnp.where(member, found[a * LOWS : (a + 1) * LOWS], 0.0), axis=0, keepdims=True)
        for a in range(3)
    ]
    cu = res_ref[0:1, :] + jac_ref[0:1, :] * s[0] + jac_ref[1:2, :] * s[1] + jac_ref[2:3, :] * s[2]
    cv = res_ref[1:2, :] + jac_ref[3:4, :] * s[0] + jac_ref[4:5, :] * s[1] + jac_ref[5:6, :] * s[2]
    cu = cu.astype(BF16).astype(F32)
    cv = cv.astype(BF16).astype(F32)
    terms = turned_ref[:CAMP, :].astype(F32) * cu + turned_ref[CAMP:, :].astype(F32) * cv
    top, rest = split(terms)
    right_ref[:CAMP, :] = top.astype(BF16)
    right_ref[CAMP:, :] = rest.astype(BF16)
    place = place_ref[...]
    for q in range(grad_ref.shape[0] // 256):
        left_ref[...] = one_hot(place - q * 256, 256)
        both = lax.dot_general(left_ref[...], right_ref[...], NT, preferred_element_type=F32)
        grad_ref[q * 256 : (q + 1) * 256, :] = both[:, :CAMP] + both[:, CAMP:]


def shape(dims, kind=F32):
    return jax.ShapeDtypeStruct(dims, kind)


LIMIT = pltpu.CompilerParams(vmem_limit_bytes=16 * 1024 * 1024)


def cost(flops, size):
    return pl.CostEstimate(flops=flops, bytes_accessed=size, transcendentals=0)


def exchange(value, groups):
    return lax.all_to_all(value, FLAT, 0, 0, axis_index_groups=groups, tiled=True)


def per_device(jac_point, jac_cam, resid, point_ids, cam_ids, owner_slot, damping):
    count = point_ids.shape[0]
    groups = owner_slot.shape[0]
    points = LOWS * HIGHS
    vmem = pl.BlockSpec(memory_space=pltpu.VMEM)
    pids = point_ids.reshape(count // 128, 128)
    cams = cam_ids.reshape(count // 128, 128)
    parts = pl.pallas_call(
        stats_kernel,
        out_shape=shape((OWNERS, 1, 9 * OWNED)),
        in_specs=[vmem] * 3,
        out_specs=vmem,
        scratch_shapes=[pltpu.VMEM((HIGHS, count), BF16), pltpu.VMEM((18 * LOWS, count), BF16)],
        name="stats",
    )(jac_point, resid, pids)
    parts = exchange(parts, CLOSE_GROUPS)
    parts, pids, cams, owner_slot, jac_cam, damping = lax.optimization_barrier(
        (parts, pids, cams, owner_slot, jac_cam, damping)
    )
    parts = pl.pallas_call(
        gather_kernel,
        out_shape=shape((OWNERS, 1, 9 * OWNED)),
        in_specs=[vmem],
        out_specs=vmem,
        compiler_params=LIMIT,
        name="gather",
    )(parts)
    arrived = exchange(parts, LINE_GROUPS)
    hot, place, turned = pl.pallas_call(
        prepare_kernel,
        out_shape=(shape((HIGHS, count), BF16), shape((1, count), jnp.int32), shape((2 * CAMP, count), BF16)),
        in_specs=[vmem] * 4,
        out_specs=(vmem, vmem, vmem),
        cost_estimate=cost(10_000_000, 6_000_000),
        compiler_params=LIMIT,
        name="prepare",
    )(pids, cams, owner_slot.reshape(8, groups // 8), jac_cam)
    arrived, hot, place, turned = lax.optimization_barrier((arrived, hot, place, turned))
    steps = pl.pallas_call(
        solve_kernel,
        out_shape=shape((OWNERS, 1, 3 * OWNED)),
        in_specs=[vmem, vmem],
        out_specs=vmem,
        compiler_params=LIMIT,
        name="solve",
    )(damping.reshape(1, 1), arrived)
    steps = exchange(steps, CLOSE_GROUPS)
    step, partial_grad = pl.pallas_call(
        camera_kernel,
        out_shape=(shape((3, points)), shape((groups, CAMP))),
        in_specs=[vmem] * 7,
        out_specs=(vmem, vmem),
        scratch_shapes=[pltpu.VMEM((2 * CAMP, count), BF16), pltpu.VMEM((256, count), BF16), pltpu.VMEM((3 * LOWS, HIGHS), F32)],
        compiler_params=LIMIT,
        name="camera",
    )(steps, jac_point, resid, pids, hot, place, turned)
    near = exchange(partial_grad.reshape(32, 32, CAMP), NEAR_GROUPS)
    near = jnp.sum(near, axis=0)
    far = exchange(near.reshape(16, 2, CAMP), FAR_GROUPS)
    return (step, jnp.sum(far, axis=0))


def solution(mesh):
    placed = (P(None, FLAT), P(FLAT, None), P(None, FLAT), P(FLAT), P(FLAT), P(), P())
    return jax.shard_map(
        per_device,
        mesh=mesh,
        in_specs=placed,
        out_specs=(P(None, "lm"), P(FLAT, None)),
        check_vma=False,
    )
```

```python
import jax
import jax.numpy as jnp
import numpy as np
from jax import lax
from jax.experimental import pallas as pl
from jax.experimental.pallas import tpu as pltpu
from jax.sharding import Mesh
from jax.sharding import PartitionSpec as P

CAMP = 128
IMG = ("y", "z")
LM = ("x", "c")
ALL = ("y", "z", "x", "c")
FLAT = ("img", "lm")
GRID = np.arange(512).reshape(4, 16, 4, 2)
TURNED = GRID[[2, 3, 0, 1]][:, [z ^ 8 for z in range(16)]][:, :, [2, 3, 0, 1]]
PAIRS = TURNED.reshape(4, 8, 2, 4, 2)
CLOSE_GROUPS = [PAIRS[:, z, :, x, c].reshape(-1).tolist() for z in range(8) for x in range(4) for c in range(2)]
LINE_GROUPS = [PAIRS[y, :, z, x, c].tolist() for y in range(4) for z in range(2) for x in range(4) for c in range(2)]
NEAR_GROUPS = [TURNED[:, z].reshape(-1).tolist() for z in range(16)]
FAR_GROUPS = [TURNED[y, :, x, c].tolist() for y in range(4) for x in range(4) for c in range(2)]
F32 = jnp.float32
BF16 = jnp.bfloat16

LOWS = 16
HIGHS = 256
OWNERS = 8
OWNED = 512
NT = (((1,), (1,)), ((), ()))


def split(value):
    top = value.astype(BF16).astype(F32)
    return top, value - top


def row_of(ref):
    return jnp.concatenate([ref[i : i + 1, :] for i in range(ref.shape[0])], axis=1)


def one_hot(row, count):
    index = lax.broadcasted_iota(jnp.int32, (count, row.shape[1]), 0).astype(F32).astype(BF16)
    row = jnp.clip(row, -1, 256).astype(F32).astype(BF16)
    return jnp.where(index == row, jnp.ones((), BF16), jnp.zeros((), BF16))


def stats_kernel(jac_ref, res_ref, pid_ref, out_ref, hot_ref, terms_ref):
    pid = row_of(pid_ref)
    hot_ref[...] = one_hot(pid & 255, HIGHS)
    low = lax.shift_right_logical(pid, 8)
    u = [jac_ref[a : a + 1, :] for a in range(3)]
    v = [jac_ref[a : a + 1, :] for a in range(3, 6)]
    ru, rv = res_ref[0:1, :], res_ref[1:2, :]
    terms = [u[a] * u[b] + v[a] * v[b] for a, b in ((0, 0), (0, 1), (0, 2), (1, 1), (1, 2), (2, 2))]
    terms += [u[a] * ru + v[a] * rv for a in range(3)]
    member = lax.broadcasted_iota(jnp.int32, (LOWS, pid.shape[1]), 0) == low
    for i, term in enumerate(terms):
        for j, piece in enumerate(split(term)):
            at = (j * 9 + i) * LOWS
            terms_ref[at : at + LOWS, :] = jnp.where(member, piece, 0.0).astype(BF16)
    both = lax.dot_general(terms_ref[...], hot_ref[...], NT, preferred_element_type=F32)
    stats = both[: 9 * LOWS] + both[9 * LOWS :]
    for v in range(9):
        for low in range(LOWS):
            at = v * OWNED + (low % 2) * HIGHS
            row = v * LOWS + low
            out_ref[low // 2, :, at : at + HIGHS] = stats[row : row + 1, :]


def prepare_kernel(pid_ref, cam_ref, slot_ref, jac_ref, hot_ref, place_ref, turned_ref):
    hot_ref[...] = one_hot(row_of(pid_ref) & 255, HIGHS)
    cam = row_of(cam_ref)
    hot = one_hot(cam & 127, 128)
    slot = slot_ref[...]
    y, z, x = (slot >> 8) ^ 2, ((slot >> 4) & 15) ^ 8, ((slot >> 1) & 7) ^ 4
    above, below = y * 8 + x, z * 2 + (slot & 1)
    table = jnp.concatenate([above, below], axis=0).astype(F32).astype(BF16)
    found = jnp.dot(table, hot, preferred_element_type=F32)
    member = lax.broadcasted_iota(jnp.int32, (8, cam.shape[1]), 0) == (cam >> 7)
    places = jnp.where(member, found[:8] * 32.0 + found[8:], 0.0)
    place_ref[...] = jnp.sum(places, axis=0, keepdims=True).astype(jnp.int32)
    turned_ref[...] = jac_ref[...].T


def total_of(parts_ref):
    total = parts_ref[0]
    for i in range(1, OWNERS):
        total = total + parts_ref[i]
    return total


def gather_kernel(damp_ref, parts_ref, out_ref, factor_ref):
    out_ref[...] = jnp.broadcast_to(total_of(parts_ref)[None], out_ref.shape)
    factor_ref[...] = jnp.broadcast_to(damp_ref[...], factor_ref.shape)


def solve_kernel(factor_ref, parts_ref, out_ref):
    total = total_of(parts_ref)
    s = [total[:, v * OWNED : (v + 1) * OWNED] for v in range(9)]
    factor = factor_ref[...]
    h01, h02, h12 = s[1], s[2], s[4]
    a00 = s[0] + factor * (s[0] + 1.0)
    a11 = s[3] + factor * (s[3] + 1.0)
    a22 = s[5] + factor * (s[5] + 1.0)
    g0, g1, g2 = s[6], s[7], s[8]
    c00 = a11 * a22 - h12 * h12
    c01 = h02 * h12 - h01 * a22
    c02 = h01 * h12 - h02 * a11
    c11 = a00 * a22 - h02 * h02
    c12 = h01 * h02 - a00 * h12
    c22 = a00 * a11 - h01 * h01
    determ = a00 * c00 + h01 * c01 + h02 * c02
    s0 = -(c00 * g0 + c01 * g1 + c02 * g2) / determ
    s1 = -(c01 * g0 + c11 * g1 + c12 * g2) / determ
    s2 = -(c02 * g0 + c12 * g1 + c22 * g2) / determ
    out_ref[...] = jnp.broadcast_to(jnp.concatenate([s0, s1, s2], axis=1)[None], out_ref.shape)


def camera_kernel(
    steps_ref, jac_ref, res_ref, pid_ref, hot_ref, place_ref, turned_ref, step_ref, grad_ref, right_ref, left_ref, table_ref
):
    for axis in range(3):
        for low in range(LOWS):
            at = axis * OWNED + (low % 2) * HIGHS
            row = steps_ref[low // 2, :, at : at + HIGHS]
            table_ref[axis * LOWS + low : axis * LOWS + low + 1, :] = row
            step_ref[axis : axis + 1, low * HIGHS : (low + 1) * HIGHS] = row
    table = table_ref[...]
    top, rest = split(table)
    table = jnp.concatenate([top, rest], axis=0).astype(BF16)
    found = jnp.dot(table, hot_ref[...], preferred_element_type=F32)
    found = found[: 3 * LOWS] + found[3 * LOWS :]
    pid = row_of(pid_ref)
    member = lax.broadcasted_iota(jnp.int32, (LOWS, pid.shape[1]), 0) == lax.shift_right_logical(pid, 8)
    s = [
        jnp.sum(jnp.where(member, found[a * LOWS : (a + 1) * LOWS], 0.0), axis=0, keepdims=True)
        for a in range(3)
    ]
    cu = res_ref[0:1, :] + jac_ref[0:1, :] * s[0] + jac_ref[1:2, :] * s[1] + jac_ref[2:3, :] * s[2]
    cv = res_ref[1:2, :] + jac_ref[3:4, :] * s[0] + jac_ref[4:5, :] * s[1] + jac_ref[5:6, :] * s[2]
    cu = cu.astype(BF16).astype(F32)
    cv = cv.astype(BF16).astype(F32)
    terms = turned_ref[:CAMP, :].astype(F32) * cu + turned_ref[CAMP:, :].astype(F32) * cv
    top, rest = split(terms)
    right_ref[:CAMP, :] = top.astype(BF16)
    right_ref[CAMP:, :] = rest.astype(BF16)
    place = place_ref[...]
    for q in range(grad_ref.shape[0] // 256):
        left_ref[...] = one_hot(place - q * 256, 256)
        both = lax.dot_general(left_ref[...], right_ref[...], NT, preferred_element_type=F32)
        grad_ref[q * 256 : (q + 1) * 256, :] = both[:, :CAMP] + both[:, CAMP:]


def shape(dims, kind=F32):
    return jax.ShapeDtypeStruct(dims, kind)


LIMIT = pltpu.CompilerParams(vmem_limit_bytes=16 * 1024 * 1024)


def cost(flops, size):
    return pl.CostEstimate(flops=flops, bytes_accessed=size, transcendentals=0)


def exchange(value, groups):
    return lax.all_to_all(value, FLAT, 0, 0, axis_index_groups=groups, tiled=True)


def per_device(jac_point, jac_cam, resid, point_ids, cam_ids, owner_slot, damping):
    count = point_ids.shape[0]
    groups = owner_slot.shape[0]
    points = LOWS * HIGHS
    vmem = pl.BlockSpec(memory_space=pltpu.VMEM)
    pids = point_ids.reshape(count // 128, 128)
    cams = cam_ids.reshape(count // 128, 128)
    parts = pl.pallas_call(
        stats_kernel,
        out_shape=shape((OWNERS, 1, 9 * OWNED)),
        in_specs=[vmem] * 3,
        out_specs=vmem,
        scratch_shapes=[pltpu.VMEM((HIGHS, count), BF16), pltpu.VMEM((18 * LOWS, count), BF16)],
        name="stats",
    )(jac_point, resid, pids)
    parts = exchange(parts, CLOSE_GROUPS)
    hot, place, turned = pl.pallas_call(
        prepare_kernel,
        out_shape=(shape((HIGHS, count), BF16), shape((1, count), jnp.int32), shape((2 * CAMP, count), BF16)),
        in_specs=[vmem] * 4,
        out_specs=(vmem, vmem, vmem),
        cost_estimate=cost(10_000_000, 6_000_000),
        compiler_params=LIMIT,
        name="prepare",
    )(pids, cams, owner_slot.reshape(8, groups // 8), jac_cam)
    parts, hot, place, turned = lax.optimization_barrier((parts, hot, place, turned))
    parts, factor = pl.pallas_call(
        gather_kernel,
        out_shape=(shape((OWNERS, 1, 9 * OWNED)), shape((1, OWNED))),
        in_specs=[vmem] * 2,
        out_specs=(vmem, vmem),
        compiler_params=LIMIT,
        name="gather",
    )(damping.reshape(1, 1), parts)
    arrived = exchange(parts, LINE_GROUPS)
    steps = pl.pallas_call(
        solve_kernel,
        out_shape=shape((OWNERS, 1, 3 * OWNED)),
        in_specs=[vmem, vmem],
        out_specs=vmem,
        compiler_params=LIMIT,
        name="solve",
    )(factor, arrived)
    steps = exchange(steps, CLOSE_GROUPS)
    step, partial_grad = pl.pallas_call(
        camera_kernel,
        out_shape=(shape((3, points)), shape((groups, CAMP))),
        in_specs=[vmem] * 7,
        out_specs=(vmem, vmem),
        scratch_shapes=[pltpu.VMEM((2 * CAMP, count), BF16), pltpu.VMEM((256, count), BF16), pltpu.VMEM((3 * LOWS, HIGHS), F32)],
        compiler_params=LIMIT,
        name="camera",
    )(steps, jac_point, resid, pids, hot, place, turned)
    near = exchange(partial_grad.reshape(32, 32, CAMP), NEAR_GROUPS)
    near = jnp.sum(near, axis=0)
    far = exchange(near.reshape(16, 2, CAMP), FAR_GROUPS)
    return (step, jnp.sum(far, axis=0))


def solution(mesh):
    placed = (P(None, FLAT), P(FLAT, None), P(None, FLAT), P(FLAT), P(FLAT), P(), P())
    return jax.shard_map(
        per_device,
        mesh=mesh,
        in_specs=placed,
        out_specs=(P(None, "lm"), P(FLAT, None)),
        check_vma=False,
    )
```

```python
import jax
import jax.numpy as jnp
import numpy as np
from jax import lax
from jax.experimental import pallas as pl
from jax.experimental.pallas import tpu as pltpu
from jax.sharding import Mesh
from jax.sharding import PartitionSpec as P

CAMP = 128
IMG = ("y", "z")
LM = ("x", "c")
ALL = ("y", "z", "x", "c")
FLAT = ("img", "lm")
GRID = np.arange(512).reshape(4, 16, 4, 2)
TURNED = GRID[[2, 3, 0, 1]][:, [z ^ 8 for z in range(16)]][:, :, [2, 3, 0, 1], ::-1]
PAIRS = TURNED.reshape(4, 8, 2, 4, 2)
CLOSE_GROUPS = [PAIRS[:, z, :, x, c].T.reshape(-1).tolist() for z in range(8) for x in range(4) for c in range(2)]
LINE_GROUPS = [PAIRS[y, :, z, x, c].tolist() for y in range(4) for z in range(2) for x in range(4) for c in range(2)]
NEAR_GROUPS = [TURNED[:, z].reshape(-1).tolist() for z in range(16)]
FAR_GROUPS = [TURNED[y, :, x, c].tolist() for y in range(4) for x in range(4) for c in range(2)]
F32 = jnp.float32
BF16 = jnp.bfloat16

LOWS = 16
HIGHS = 256
OWNERS = 8
OWNED = 512
NT = (((1,), (1,)), ((), ()))


def split(value):
    top = value.astype(BF16).astype(F32)
    return top, value - top


def row_of(ref):
    return jnp.concatenate([ref[i : i + 1, :] for i in range(ref.shape[0])], axis=1)


def one_hot(row, count):
    index = lax.broadcasted_iota(jnp.int32, (count, row.shape[1]), 0).astype(F32).astype(BF16)
    row = jnp.clip(row, -1, 256).astype(F32).astype(BF16)
    return jnp.where(index == row, jnp.ones((), BF16), jnp.zeros((), BF16))


def stats_kernel(jac_ref, res_ref, pid_ref, out_ref, hot_ref, terms_ref):
    pid = row_of(pid_ref)
    hot_ref[...] = one_hot(pid & 255, HIGHS)
    low = lax.shift_right_logical(pid, 8)
    u = [jac_ref[a : a + 1, :] for a in range(3)]
    v = [jac_ref[a : a + 1, :] for a in range(3, 6)]
    ru, rv = res_ref[0:1, :], res_ref[1:2, :]
    terms = [u[a] * u[b] + v[a] * v[b] for a, b in ((0, 0), (0, 1), (0, 2), (1, 1), (1, 2), (2, 2))]
    terms += [u[a] * ru + v[a] * rv for a in range(3)]
    member = lax.broadcasted_iota(jnp.int32, (LOWS, pid.shape[1]), 0) == low
    for i, term in enumerate(terms):
        for j, piece in enumerate(split(term)):
            at = (j * 9 + i) * LOWS
            terms_ref[at : at + LOWS, :] = jnp.where(member, piece, 0.0).astype(BF16)
    both = lax.dot_general(terms_ref[...], hot_ref[...], NT, preferred_element_type=F32)
    stats = both[: 9 * LOWS] + both[9 * LOWS :]
    for v in range(9):
        for low in range(LOWS):
            at = v * OWNED + (low % 2) * HIGHS
            row = v * LOWS + low
            out_ref[low // 2, :, at : at + HIGHS] = stats[row : row + 1, :]


def prepare_kernel(pid_ref, cam_ref, slot_ref, jac_ref, hot_ref, place_ref, turned_ref):
    hot_ref[...] = one_hot(row_of(pid_ref) & 255, HIGHS)
    cam = row_of(cam_ref)
    hot = one_hot(cam & 127, 128)
    slot = slot_ref[...]
    y, z, x = (slot >> 8) ^ 2, ((slot >> 4) & 15) ^ 8, ((slot >> 1) & 7) ^ 5
    above, below = y * 8 + x, z * 2 + (slot & 1)
    table = jnp.concatenate([above, below], axis=0).astype(F32).astype(BF16)
    found = jnp.dot(table, hot, preferred_element_type=F32)
    member = lax.broadcasted_iota(jnp.int32, (8, cam.shape[1]), 0) == (cam >> 7)
    places = jnp.where(member, found[:8] * 32.0 + found[8:], 0.0)
    place_ref[...] = jnp.sum(places, axis=0, keepdims=True).astype(jnp.int32)
    turned_ref[...] = jac_ref[...].T


def total_of(parts_ref):
    total = parts_ref[0]
    for i in range(1, OWNERS):
        total = total + parts_ref[i]
    return total


def gather_kernel(damp_ref, parts_ref, out_ref, factor_ref):
    out_ref[...] = jnp.broadcast_to(total_of(parts_ref)[None], out_ref.shape)
    factor_ref[...] = jnp.broadcast_to(damp_ref[...], factor_ref.shape)


def solve_kernel(factor_ref, parts_ref, out_ref):
    total = total_of(parts_ref)
    s = [total[:, v * OWNED : (v + 1) * OWNED] for v in range(9)]
    factor = factor_ref[...]
    h01, h02, h12 = s[1], s[2], s[4]
    a00 = s[0] + factor * (s[0] + 1.0)
    a11 = s[3] + factor * (s[3] + 1.0)
    a22 = s[5] + factor * (s[5] + 1.0)
    g0, g1, g2 = s[6], s[7], s[8]
    c00 = a11 * a22 - h12 * h12
    c01 = h02 * h12 - h01 * a22
    c02 = h01 * h12 - h02 * a11
    c11 = a00 * a22 - h02 * h02
    c12 = h01 * h02 - a00 * h12
    c22 = a00 * a11 - h01 * h01
    determ = a00 * c00 + h01 * c01 + h02 * c02
    s0 = -(c00 * g0 + c01 * g1 + c02 * g2) / determ
    s1 = -(c01 * g0 + c11 * g1 + c12 * g2) / determ
    s2 = -(c02 * g0 + c12 * g1 + c22 * g2) / determ
    out_ref[...] = jnp.broadcast_to(jnp.concatenate([s0, s1, s2], axis=1)[None], out_ref.shape)


def camera_kernel(
    steps_ref, jac_ref, res_ref, pid_ref, hot_ref, place_ref, turned_ref, step_ref, grad_ref, right_ref, left_ref, table_ref
):
    for axis in range(3):
        for low in range(LOWS):
            at = axis * OWNED + (low % 2) * HIGHS
            row = steps_ref[low // 2, :, at : at + HIGHS]
            table_ref[axis * LOWS + low : axis * LOWS + low + 1, :] = row
            step_ref[axis : axis + 1, low * HIGHS : (low + 1) * HIGHS] = row
    table = table_ref[...]
    top, rest = split(table)
    table = jnp.concatenate([top, rest], axis=0).astype(BF16)
    found = jnp.dot(table, hot_ref[...], preferred_element_type=F32)
    found = found[: 3 * LOWS] + found[3 * LOWS :]
    pid = row_of(pid_ref)
    member = lax.broadcasted_iota(jnp.int32, (LOWS, pid.shape[1]), 0) == lax.shift_right_logical(pid, 8)
    s = [
        jnp.sum(jnp.where(member, found[a * LOWS : (a + 1) * LOWS], 0.0), axis=0, keepdims=True)
        for a in range(3)
    ]
    cu = res_ref[0:1, :] + jac_ref[0:1, :] * s[0] + jac_ref[1:2, :] * s[1] + jac_ref[2:3, :] * s[2]
    cv = res_ref[1:2, :] + jac_ref[3:4, :] * s[0] + jac_ref[4:5, :] * s[1] + jac_ref[5:6, :] * s[2]
    cu = cu.astype(BF16).astype(F32)
    cv = cv.astype(BF16).astype(F32)
    terms = turned_ref[:CAMP, :].astype(F32) * cu + turned_ref[CAMP:, :].astype(F32) * cv
    top, rest = split(terms)
    right_ref[:CAMP, :] = top.astype(BF16)
    right_ref[CAMP:, :] = rest.astype(BF16)
    place = place_ref[...]
    for q in range(grad_ref.shape[0] // 256):
        left_ref[q * 256 : (q + 1) * 256, :] = one_hot(place - q * 256, 256)
    both = lax.dot_general(left_ref[...], right_ref[...], NT, preferred_element_type=F32)
    grad_ref[...] = both[:, :CAMP] + both[:, CAMP:]


def shape(dims, kind=F32):
    return jax.ShapeDtypeStruct(dims, kind)


LIMIT = pltpu.CompilerParams(vmem_limit_bytes=16 * 1024 * 1024)


def cost(flops, size):
    return pl.CostEstimate(flops=flops, bytes_accessed=size, transcendentals=0)


def exchange(value, groups):
    return lax.all_to_all(value, FLAT, 0, 0, axis_index_groups=groups, tiled=True)


def per_device(jac_point, jac_cam, resid, point_ids, cam_ids, owner_slot, damping):
    count = point_ids.shape[0]
    groups = owner_slot.shape[0]
    points = LOWS * HIGHS
    vmem = pl.BlockSpec(memory_space=pltpu.VMEM)
    pids = point_ids.reshape(count // 128, 128)
    cams = cam_ids.reshape(count // 128, 128)
    parts = pl.pallas_call(
        stats_kernel,
        out_shape=shape((OWNERS, 1, 9 * OWNED)),
        in_specs=[vmem] * 3,
        out_specs=vmem,
        scratch_shapes=[pltpu.VMEM((HIGHS, count), BF16), pltpu.VMEM((18 * LOWS, count), BF16)],
        name="stats",
    )(jac_point, resid, pids)
    parts = exchange(parts, CLOSE_GROUPS)
    hot, place, turned = pl.pallas_call(
        prepare_kernel,
        out_shape=(shape((HIGHS, count), BF16), shape((1, count), jnp.int32), shape((2 * CAMP, count), BF16)),
        in_specs=[vmem] * 4,
        out_specs=(vmem, vmem, vmem),
        cost_estimate=cost(10_000_000, 6_000_000),
        compiler_params=LIMIT,
        name="prepare",
    )(pids, cams, owner_slot.reshape(8, groups // 8), jac_cam)
    parts, hot, place, turned = lax.optimization_barrier((parts, hot, place, turned))
    parts, factor = pl.pallas_call(
        gather_kernel,
        out_shape=(shape((OWNERS, 1, 9 * OWNED)), shape((1, OWNED))),
        in_specs=[vmem] * 2,
        out_specs=(vmem, vmem),
        compiler_params=LIMIT,
        name="gather",
    )(damping.reshape(1, 1), parts)
    arrived = exchange(parts, LINE_GROUPS)
    steps = pl.pallas_call(
        solve_kernel,
        out_shape=shape((OWNERS, 1, 3 * OWNED)),
        in_specs=[vmem, vmem],
        out_specs=vmem,
        compiler_params=LIMIT,
        name="solve",
    )(factor, arrived)
    steps = exchange(steps, CLOSE_GROUPS)
    step, partial_grad = pl.pallas_call(
        camera_kernel,
        out_shape=(shape((3, points)), shape((groups, CAMP))),
        in_specs=[vmem] * 7,
        out_specs=(vmem, vmem),
        scratch_shapes=[pltpu.VMEM((2 * CAMP, count), BF16), pltpu.VMEM((groups, count), BF16), pltpu.VMEM((3 * LOWS, HIGHS), F32)],
        compiler_params=LIMIT,
        name="camera",
    )(steps, jac_point, resid, pids, hot, place, turned)
    near = exchange(partial_grad.reshape(32, 32, CAMP), NEAR_GROUPS)
    near = jnp.sum(near, axis=0)
    far = exchange(near.reshape(16, 2, CAMP), FAR_GROUPS)
    return (step, jnp.sum(far, axis=0))


def solution(mesh):
    placed = (P(None, FLAT), P(FLAT, None), P(None, FLAT), P(FLAT), P(FLAT), P(), P())
    return jax.shard_map(
        per_device,
        mesh=mesh,
        in_specs=placed,
        out_specs=(P(None, "lm"), P(FLAT, None)),
        check_vma=False,
    )
```

```python
import jax
import jax.numpy as jnp
import numpy as np
from jax import lax
from jax.experimental import pallas as pl
from jax.experimental.pallas import tpu as pltpu
from jax.sharding import Mesh
from jax.sharding import PartitionSpec as P

CAMP = 128
IMG = ("y", "z")
LM = ("x", "c")
ALL = ("y", "z", "x", "c")
FLAT = ("img", "lm")
GRID = np.arange(512).reshape(4, 16, 4, 2)
TURNED = GRID[[2, 3, 0, 1]][:, [(z + 10) % 16 for z in range(16)]][:, :, [2, 3, 0, 1], ::-1]
PAIRS = TURNED.reshape(4, 8, 2, 4, 2)
CLOSE_GROUPS = [PAIRS[:, z, :, x, c].T.reshape(-1).tolist() for z in range(8) for x in range(4) for c in range(2)]
LINE_GROUPS = [PAIRS[y, :, z, x, c].tolist() for y in range(4) for z in range(2) for x in range(4) for c in range(2)]
NEAR_GROUPS = [TURNED[:, z].reshape(-1).tolist() for z in range(16)]
FAR_GROUPS = [TURNED[y, :, x, c].tolist() for y in range(4) for x in range(4) for c in range(2)]
F32 = jnp.float32
BF16 = jnp.bfloat16

LOWS = 16
HIGHS = 256
OWNERS = 8
OWNED = 512
NT = (((1,), (1,)), ((), ()))


def split(value):
    top = value.astype(BF16).astype(F32)
    return top, value - top


def row_of(ref):
    return jnp.concatenate([ref[i : i + 1, :] for i in range(ref.shape[0])], axis=1)


def one_hot(row, count):
    index = lax.broadcasted_iota(jnp.int32, (count, row.shape[1]), 0).astype(F32).astype(BF16)
    row = jnp.clip(row, -1, 256).astype(F32).astype(BF16)
    return jnp.where(index == row, jnp.ones((), BF16), jnp.zeros((), BF16))


def stats_kernel(jac_ref, res_ref, pid_ref, out_ref, hot_ref, terms_ref):
    pid = row_of(pid_ref)
    hot_ref[...] = one_hot(pid & 255, HIGHS)
    low = lax.shift_right_logical(pid, 8)
    u = [jac_ref[a : a + 1, :] for a in range(3)]
    v = [jac_ref[a : a + 1, :] for a in range(3, 6)]
    ru, rv = res_ref[0:1, :], res_ref[1:2, :]
    terms = [u[a] * u[b] + v[a] * v[b] for a, b in ((0, 0), (0, 1), (0, 2), (1, 1), (1, 2), (2, 2))]
    terms += [u[a] * ru + v[a] * rv for a in range(3)]
    member = lax.broadcasted_iota(jnp.int32, (LOWS, pid.shape[1]), 0) == low
    for i, term in enumerate(terms):
        for j, piece in enumerate(split(term)):
            at = (j * 9 + i) * LOWS
            terms_ref[at : at + LOWS, :] = jnp.where(member, piece, 0.0).astype(BF16)
    both = lax.dot_general(terms_ref[...], hot_ref[...], NT, preferred_element_type=F32)
    stats = both[: 9 * LOWS] + both[9 * LOWS :]
    for v in range(9):
        for low in range(LOWS):
            at = v * OWNED + (low % 2) * HIGHS
            row = v * LOWS + low
            out_ref[low // 2, :, at : at + HIGHS] = stats[row : row + 1, :]


def prepare_kernel(pid_ref, cam_ref, slot_ref, jac_ref, hot_ref, place_ref, turned_ref):
    hot_ref[...] = one_hot(row_of(pid_ref) & 255, HIGHS)
    cam = row_of(cam_ref)
    hot = one_hot(cam & 127, 128)
    slot = slot_ref[...]
    y, z, x = ((slot >> 8) - 2) & 3, ((slot >> 4) - 10) & 15, ((slot >> 1) & 7) ^ 5
    above, below = y * 8 + x, z * 2 + (slot & 1)
    table = jnp.concatenate([above, below], axis=0).astype(F32).astype(BF16)
    found = jnp.dot(table, hot, preferred_element_type=F32)
    member = lax.broadcasted_iota(jnp.int32, (8, cam.shape[1]), 0) == (cam >> 7)
    places = jnp.where(member, found[:8] * 32.0 + found[8:], 0.0)
    place_ref[...] = jnp.sum(places, axis=0, keepdims=True).astype(jnp.int32)
    turned_ref[...] = jac_ref[...].T


def total_of(parts_ref):
    total = parts_ref[0]
    for i in range(1, OWNERS):
        total = total + parts_ref[i]
    return total


def gather_kernel(damp_ref, parts_ref, out_ref, factor_ref):
    out_ref[...] = jnp.broadcast_to(total_of(parts_ref)[None], out_ref.shape)
    factor_ref[...] = jnp.broadcast_to(damp_ref[...], factor_ref.shape)


def solve_kernel(factor_ref, parts_ref, out_ref):
    total = total_of(parts_ref)
    s = [total[:, v * OWNED : (v + 1) * OWNED] for v in range(9)]
    factor = factor_ref[...]
    h01, h02, h12 = s[1], s[2], s[4]
    a00 = s[0] + factor * (s[0] + 1.0)
    a11 = s[3] + factor * (s[3] + 1.0)
    a22 = s[5] + factor * (s[5] + 1.0)
    g0, g1, g2 = s[6], s[7], s[8]
    c00 = a11 * a22 - h12 * h12
    c01 = h02 * h12 - h01 * a22
    c02 = h01 * h12 - h02 * a11
    c11 = a00 * a22 - h02 * h02
    c12 = h01 * h02 - a00 * h12
    c22 = a00 * a11 - h01 * h01
    determ = a00 * c00 + h01 * c01 + h02 * c02
    s0 = -(c00 * g0 + c01 * g1 + c02 * g2) / determ
    s1 = -(c01 * g0 + c11 * g1 + c12 * g2) / determ
    s2 = -(c02 * g0 + c12 * g1 + c22 * g2) / determ
    out_ref[...] = jnp.broadcast_to(jnp.concatenate([s0, s1, s2], axis=1)[None], out_ref.shape)


def camera_kernel(
    steps_ref, jac_ref, res_ref, pid_ref, hot_ref, place_ref, turned_ref, step_ref, grad_ref, right_ref, left_ref, table_ref
):
    for axis in range(3):
        for low in range(LOWS):
            at = axis * OWNED + (low % 2) * HIGHS
            row = steps_ref[low // 2, :, at : at + HIGHS]
            table_ref[axis * LOWS + low : axis * LOWS + low + 1, :] = row
            step_ref[axis : axis + 1, low * HIGHS : (low + 1) * HIGHS] = row
    table = table_ref[...]
    top, rest = split(table)
    table = jnp.concatenate([top, rest], axis=0).astype(BF16)
    found = jnp.dot(table, hot_ref[...], preferred_element_type=F32)
    found = found[: 3 * LOWS] + found[3 * LOWS :]
    pid = row_of(pid_ref)
    member = lax.broadcasted_iota(jnp.int32, (LOWS, pid.shape[1]), 0) == lax.shift_right_logical(pid, 8)
    s = [
        jnp.sum(jnp.where(member, found[a * LOWS : (a + 1) * LOWS], 0.0), axis=0, keepdims=True)
        for a in range(3)
    ]
    cu = res_ref[0:1, :] + jac_ref[0:1, :] * s[0] + jac_ref[1:2, :] * s[1] + jac_ref[2:3, :] * s[2]
    cv = res_ref[1:2, :] + jac_ref[3:4, :] * s[0] + jac_ref[4:5, :] * s[1] + jac_ref[5:6, :] * s[2]
    cu = cu.astype(BF16).astype(F32)
    cv = cv.astype(BF16).astype(F32)
    terms = turned_ref[:CAMP, :].astype(F32) * cu + turned_ref[CAMP:, :].astype(F32) * cv
    top, rest = split(terms)
    right_ref[:CAMP, :] = top.astype(BF16)
    right_ref[CAMP:, :] = rest.astype(BF16)
    place = place_ref[...]
    for q in range(grad_ref.shape[0] // 256):
        left_ref[q * 256 : (q + 1) * 256, :] = one_hot(place - q * 256, 256)
    both = lax.dot_general(left_ref[...], right_ref[...], NT, preferred_element_type=F32)
    grad_ref[...] = both[:, :CAMP] + both[:, CAMP:]


def shape(dims, kind=F32):
    return jax.ShapeDtypeStruct(dims, kind)


LIMIT = pltpu.CompilerParams(vmem_limit_bytes=16 * 1024 * 1024)


def cost(flops, size):
    return pl.CostEstimate(flops=flops, bytes_accessed=size, transcendentals=0)


def exchange(value, groups):
    return lax.all_to_all(value, FLAT, 0, 0, axis_index_groups=groups, tiled=True)


def per_device(jac_point, jac_cam, resid, point_ids, cam_ids, owner_slot, damping):
    count = point_ids.shape[0]
    groups = owner_slot.shape[0]
    points = LOWS * HIGHS
    vmem = pl.BlockSpec(memory_space=pltpu.VMEM)
    pids = point_ids.reshape(count // 128, 128)
    cams = cam_ids.reshape(count // 128, 128)
    parts = pl.pallas_call(
        stats_kernel,
        out_shape=shape((OWNERS, 1, 9 * OWNED)),
        in_specs=[vmem] * 3,
        out_specs=vmem,
        scratch_shapes=[pltpu.VMEM((HIGHS, count), BF16), pltpu.VMEM((18 * LOWS, count), BF16)],
        name="stats",
    )(jac_point, resid, pids)
    parts = exchange(parts, CLOSE_GROUPS)
    hot, place, turned = pl.pallas_call(
        prepare_kernel,
        out_shape=(shape((HIGHS, count), BF16), shape((1, count), jnp.int32), shape((2 * CAMP, count), BF16)),
        in_specs=[vmem] * 4,
        out_specs=(vmem, vmem, vmem),
        cost_estimate=cost(10_000_000, 6_000_000),
        compiler_params=LIMIT,
        name="prepare",
    )(pids, cams, owner_slot.reshape(8, groups // 8), jac_cam)
    parts, hot, place, turned = lax.optimization_barrier((parts, hot, place, turned))
    parts, factor = pl.pallas_call(
        gather_kernel,
        out_shape=(shape((OWNERS, 1, 9 * OWNED)), shape((1, OWNED))),
        in_specs=[vmem] * 2,
        out_specs=(vmem, vmem),
        compiler_params=LIMIT,
        name="gather",
    )(damping.reshape(1, 1), parts)
    arrived = exchange(parts, LINE_GROUPS)
    steps = pl.pallas_call(
        solve_kernel,
        out_shape=shape((OWNERS, 1, 3 * OWNED)),
        in_specs=[vmem, vmem],
        out_specs=vmem,
        compiler_params=LIMIT,
        name="solve",
    )(factor, arrived)
    steps = exchange(steps, CLOSE_GROUPS)
    step, partial_grad = pl.pallas_call(
        camera_kernel,
        out_shape=(shape((3, points)), shape((groups, CAMP))),
        in_specs=[vmem] * 7,
        out_specs=(vmem, vmem),
        scratch_shapes=[pltpu.VMEM((2 * CAMP, count), BF16), pltpu.VMEM((groups, count), BF16), pltpu.VMEM((3 * LOWS, HIGHS), F32)],
        compiler_params=LIMIT,
        name="camera",
    )(steps, jac_point, resid, pids, hot, place, turned)
    near = exchange(partial_grad.reshape(32, 32, CAMP), NEAR_GROUPS)
    near = jnp.sum(near, axis=0)
    far = exchange(near.reshape(16, 2, CAMP), FAR_GROUPS)
    return (step, jnp.sum(far, axis=0))


def solution(mesh):
    placed = (P(None, FLAT), P(FLAT, None), P(None, FLAT), P(FLAT), P(FLAT), P(), P())
    return jax.shard_map(
        per_device,
        mesh=mesh,
        in_specs=placed,
        out_specs=(P(None, "lm"), P(FLAT, None)),
        check_vma=False,
    )
```
